32 devices in a mesh: rows: 16 (over z, y, x), grid: 2 (over core).
Axes of the slice: x: 2, y: 2, z: 4, core: 2. Of those that a mesh axis runs over, the one named last changes fastest.
Arguments:
- library: bfloat16 [8192, 4096], P('rows', 'grid'), may hold values from -6 to 6
- col_scale: float32 [4096], replicated, may hold values from 0.5 to 2
Outputs:
- updated: float32 [4096, 4096], P('rows', 'grid')
- reflectors: float32 [4096, 64], P('rows')
The draws below stay inside these ranges and needn't reach their ends.
All inputs are finite; a program needn't handle non-finite values.
Results may differ from the reference program's by a relative error of at most 0.0003.
Values may be sent and summed in bfloat16 or wider, within the bound.
A program may use at most 128 MiB of HBM per device.

```python
import math
import jax
import jax.numpy as jnp
from jax import lax

COLS = 4096
PANEL = 64
TOTAL_ROWS = 8192


def strengthened(entries, key, source, target, parts, factor):
    owner, partner = [(jnp.arange(entries.shape[dim]) // (entries.shape[dim] // parts)).reshape([-1 if axis == dim else 1 for axis in range(entries.ndim)]) for dim in (source, target)]
    chosen = jax.random.permutation(key, parts)[partner]
    strong = (owner == chosen) | (owner == (partner + parts // 2) % parts)
    return jnp.where(strong, factor * entries, entries)


def block_scale(key, shape, cuts, least, high):
    def one(dim, parts):
        heights = jax.random.uniform(jax.random.fold_in(jax.random.fold_in(key, 6), dim), (parts,), jnp.float32, least / len(cuts), high / len(cuts))
        return jnp.repeat(jnp.exp(heights), shape[dim] // parts).reshape((-1,) + (1,) * (len(shape) - dim - 1))

    factor_of = one(*cuts[0])
    for cut in cuts[1:]:
        factor_of = factor_of * one(*cut)
    return factor_of


def bell_draw_with(stream_key, shape, scale, most, split, heavy, held_as=jnp.bfloat16):
    drawn = scale * jax.random.normal(stream_key, shape, jnp.float32)
    if split:
        drawn = drawn * block_scale(stream_key, shape, split, -0.22, 0.18)
    return jnp.clip(strengthened(drawn, jax.random.fold_in(stream_key, 3), *heavy), -most, most).astype(held_as)


def setup_inputs(seed: int = 0) -> dict:
    arg_keys = jax.random.split(jax.random.key(seed), 3)
    return {
        "library": bell_draw_with(arg_keys[0], (TOTAL_ROWS, COLS), 1.0, 6.0, ((0, 16), (1, 2)), (0, 1, 16, 2.0)),
        "col_scale": jnp.clip(jnp.exp(jax.random.uniform(arg_keys[1], (COLS,), jnp.float32, math.log(0.5), math.log(2.0))), 0.5, 2.0),
    }


def reflect_panel(panel):
    size, width = panel.shape
    row_line = jnp.arange(size)
    col_line = jnp.arange(width)
    vectors = jnp.zeros((size, width), jnp.float32)
    factor = jnp.zeros((width, width), jnp.float32)

    def one_step(step, carry):
        work, vectors, factor = carry
        column = lax.optimization_barrier(jnp.sum(jnp.where(col_line[None, :] == step, work, 0.0), axis=1))
        column = jnp.where(row_line >= step, column, 0.0)
        pivot = jnp.sum(jnp.where(row_line == step, column, 0.0))
        length = jnp.sqrt(jnp.sum(column * column))
        sign_factor = jnp.where(pivot >= 0.0, 1.0, -1.0)
        vector = column + jnp.where(row_line == step, sign_factor * length, 0.0)
        scale = 2.0 / jnp.sum(vector * vector)
        project = jnp.dot(vector, work, precision=lax.Precision.HIGHEST)
        work = work - scale * vector[:, None] * project[None, :]
        coupling = jnp.dot(vector, vectors, precision=lax.Precision.HIGHEST)
        column_t = -scale * jnp.dot(factor, coupling, precision=lax.Precision.HIGHEST)
        column_t = column_t + jnp.where(col_line == step, scale, 0.0)
        factor = jnp.where(col_line[None, :] == step, column_t[:, None], factor)
        vectors = jnp.where(col_line[None, :] == step, vector[:, None], vectors)
        return (work, vectors, factor)
    work, vectors, factor = lax.fori_loop(0, width, one_step, (panel, vectors, factor))
    return (vectors, factor)

def reference(library, col_scale):
    total = library.shape[0]
    gram = lax.dot_general(library, library, (((0,), (0,)), ((), ())), preferred_element_type=jnp.float32)
    gram = gram * (col_scale[:, None] * col_scale[None, :] / total)
    panel = gram[:, :PANEL]
    vectors, factor = reflect_panel(panel)
    cross = jnp.dot(vectors.T, gram, precision=lax.Precision.HIGHEST)
    mixed = jnp.dot(factor.T, cross, precision=lax.Precision.HIGHEST)
    updated = gram - jnp.dot(vectors, mixed, precision=lax.Precision.HIGHEST)
    return (updated, vectors)
```

```python
import jax
import jax.numpy as jnp
from jax import lax
from jax.experimental import pallas as pl
from jax.experimental.pallas import tpu as pltpu
from jax.sharding import PartitionSpec as P

PANEL = 64
HIGH = lax.Precision.HIGHEST


def reflect_kernel(panel_ref, vectors_ref, weights_ref, work, inner, taus):
    width, size = panel_ref.shape
    lane = lax.broadcasted_iota(jnp.int32, (1, size), 1)
    work[...] = panel_ref[...]
    for base in range(0, width, 8):

        def one_step(step, carry, base=base):
            place = base + step
            row = work[pl.ds(place, 1), :]
            row = jnp.where(lane >= place, row, 0.0)
            pivot = jnp.sum(jnp.where(lane == place, row, 0.0), axis=1, keepdims=True)
            length = jnp.sqrt(jnp.sum(row * row, axis=1, keepdims=True))
            signed = jnp.where(pivot >= 0.0, length, -length)
            vector = row + jnp.where(lane == place, signed, 0.0)
            tau = 1.0 / (length * (length + jnp.abs(pivot)))
            rest = work[base:, :]
            project = jnp.sum(rest * vector, axis=1, keepdims=True)
            work[base:, :] = rest - (tau * project) * vector
            vectors_ref[pl.ds(place, 1), :] = vector
            taus[pl.ds(place, 1), :] = jnp.broadcast_to(tau, (1, 128))
            return carry

        lax.fori_loop(0, 8, one_step, 0)
    vectors = vectors_ref[...]
    inner[...] = lax.dot_general(
        vectors, vectors, (((1,), (1,)), ((), ())), precision=HIGH, preferred_element_type=jnp.float32
    )
    across = lax.broadcasted_iota(jnp.int32, (width, width), 1)
    down = lax.broadcasted_iota(jnp.int32, (width, 1), 0)

    def factor_step(place, factor):
        tau = taus[pl.ds(place, 1), 0:1]
        coupling = jnp.where(across < place, inner[pl.ds(place, 1), :] * factor, 0.0)
        column = -tau * jnp.sum(coupling, axis=1, keepdims=True)
        column = column + jnp.where(down == place, tau, 0.0)
        return jnp.where(across == place, column, factor)

    factor = lax.fori_loop(0, width, factor_step, jnp.zeros((width, width), jnp.float32))
    weights_ref[...] = lax.dot_general(
        factor, vectors, (((0,), (0,)), ((), ())), precision=HIGH, preferred_element_type=jnp.float32
    )


def reflect_panel(panel_t):
    width, size = panel_t.shape
    shape = jax.ShapeDtypeStruct((width, size), jnp.float32)
    return pl.pallas_call(
        reflect_kernel,
        out_shape=(shape, shape),
        in_specs=[pl.BlockSpec(memory_space=pltpu.VMEM)],
        out_specs=(pl.BlockSpec(memory_space=pltpu.VMEM),) * 2,
        scratch_shapes=[
            pltpu.VMEM((width, size), jnp.float32),
            pltpu.VMEM((width, width), jnp.float32),
            pltpu.VMEM((width, 128), jnp.float32),
        ],
        compiler_params=pltpu.CompilerParams(vmem_limit_bytes=16 << 20),
        cost_estimate=pl.CostEstimate(flops=20_000_000_000, bytes_accessed=100_000_000, transcendentals=0),
    )(panel_t)


def per_device(library, col_scale):
    rows_dev, col_block = library.shape
    count_rows = lax.axis_size("rows")
    count_grid = lax.axis_size("grid")
    columns = col_block * count_grid
    row_block = columns // count_rows
    total = rows_dev * count_rows
    near = 1
    while near * near < count_rows:
        near *= 2
    far = count_rows // near
    grid_place = lax.axis_index("grid")
    rows_place = lax.axis_index("rows")
    near_groups = [[f * near + n for n in range(near)] for f in range(far)]
    far_groups = [[f * near + n for f in range(far)] for n in range(near)]
    own_scale = lax.dynamic_slice_in_dim(col_scale, grid_place * col_block, col_block)

    head = lax.all_gather(library[:, :PANEL], "grid", axis=0)[0]
    panel_part = lax.dot_general(
        head, library, (((0,), (0,)), ((), ())), preferred_element_type=jnp.float32
    )
    panel_own = lax.psum(panel_part, "rows") * (col_scale[:PANEL, None] * own_scale[None, :] / total)
    panel_t = lax.all_gather(panel_own, "grid", axis=1, tiled=True)
    vectors, weights = reflect_panel(panel_t)

    whole = lax.all_gather(library, "rows", axis=0, tiled=True, axis_index_groups=near_groups)
    place = rows_place % near
    blocks = whole.reshape(near * rows_dev, far // count_grid, near, row_block)
    left = lax.dynamic_index_in_dim(blocks, place, 2, keepdims=False)
    left = lax.all_gather(left, "grid", axis=1, tiled=True).reshape(near * rows_dev, far * row_block)
    product = lax.dot_general(
        left, whole, (((0,), (0,)), ((), ())), preferred_element_type=jnp.float32
    )
    gram = lax.psum_scatter(
        product, "rows", scatter_dimension=0, tiled=True, axis_index_groups=far_groups
    )
    row_scale = lax.dynamic_slice_in_dim(col_scale, rows_place * row_block, row_block)

    scaled = weights * col_scale[None, :]
    scaled = lax.dynamic_slice_in_dim(scaled, grid_place * col_block, col_block, 1)
    wide = library.astype(jnp.float32)
    inner = lax.dot_general(scaled, wide, (((1,), (1,)), ((), ())), precision=HIGH)
    inner = lax.psum(inner, "grid")
    mixed = lax.psum(jnp.dot(inner, wide, precision=HIGH), "rows") * (own_scale[None, :] / total)
    own_vectors = lax.dynamic_slice_in_dim(vectors, rows_place * row_block, row_block, 1).T
    gram = gram * (row_scale[:, None] * own_scale[None, :] / total)
    updated = gram - jnp.dot(own_vectors, mixed, precision=HIGH)
    return (updated, own_vectors)


def solution(mesh):
    return jax.shard_map(
        per_device,
        mesh=mesh,
        in_specs=(P("rows", "grid"), P()),
        out_specs=(P("rows", "grid"), P("rows", None)),
        check_vma=False,
    )
```

```python
import functools

import jax
import jax.numpy as jnp
from jax import lax
from jax.experimental import pallas as pl
from jax.experimental.pallas import tpu as pltpu
from jax.sharding import PartitionSpec as P

PANEL = 64
HIGH = lax.Precision.HIGHEST


def reflect(vectors_ref, weights_ref, work, inner, taus):
    width, size = work.shape
    lane = lax.broadcasted_iota(jnp.int32, (1, size), 1)
    for base in range(0, width, 8):

        def one_step(step, carry, base=base):
            place = base + step
            row = work[pl.ds(place, 1), :]
            row = jnp.where(lane >= place, row, 0.0)
            pivot = jnp.sum(jnp.where(lane == place, row, 0.0), axis=1, keepdims=True)
            length = jnp.sqrt(jnp.sum(row * row, axis=1, keepdims=True))
            signed = jnp.where(pivot >= 0.0, length, -length)
            vector = row + jnp.where(lane == place, signed, 0.0)
            tau = 1.0 / (length * (length + jnp.abs(pivot)))
            rest = work[base:, :]
            project = jnp.sum(rest * vector, axis=1, keepdims=True)
            work[base:, :] = rest - (tau * project) * vector
            vectors_ref[pl.ds(place, 1), :] = vector
            taus[pl.ds(place, 1), :] = jnp.broadcast_to(tau, (1, 128))
            return carry

        lax.fori_loop(0, 8, one_step, 0)
    vectors = vectors_ref[...]
    inner[...] = lax.dot_general(
        vectors, vectors, (((1,), (1,)), ((), ())), precision=HIGH, preferred_element_type=jnp.float32
    )
    across = lax.broadcasted_iota(jnp.int32, (width, width), 1)
    down = lax.broadcasted_iota(jnp.int32, (width, 1), 0)

    def factor_step(place, factor):
        tau = taus[pl.ds(place, 1), 0:1]
        coupling = jnp.where(across < place, inner[pl.ds(place, 1), :] * factor, 0.0)
        column = -tau * jnp.sum(coupling, axis=1, keepdims=True)
        column = column + jnp.where(down == place, tau, 0.0)
        return jnp.where(across == place, column, factor)

    factor = lax.fori_loop(0, width, factor_step, jnp.zeros((width, width), jnp.float32))
    weights_ref[...] = lax.dot_general(
        factor, vectors, (((0,), (0,)), ((), ())), precision=HIGH, preferred_element_type=jnp.float32
    )


def remote(source, target, send, recv, place):
    return pltpu.make_async_remote_copy(
        src_ref=source, dst_ref=target, send_sem=send, recv_sem=recv,
        device_id=place, device_id_type=pl.DeviceIdType.MESH,
    )


def sum_rows(count, part, landed, out, sems):
    me, core = lax.axis_index("rows"), lax.axis_index("grid")
    send, recv, send_back, recv_back = sems

    def scatter(step):
        peer = lax.rem(me + step, count)
        return remote(part.at[peer], landed.at[step], send.at[step], recv.at[step], (peer, core))

    def spread(step):
        peer = lax.rem(me + step, count)
        return remote(out.at[me], out.at[me], send_back.at[step], recv_back.at[step], (peer, core))

    def arrival(step):
        peer = lax.rem(me + count - step, count)
        return remote(out.at[peer], out.at[peer], send_back.at[step], recv_back.at[step], (peer, core))

    def loop(action):
        def body(step, carry):
            action(step)
            return carry
        lax.fori_loop(1, count, body, 0)

    loop(lambda step: scatter(step).start())
    loop(lambda step: scatter(step).wait_recv())
    total = part[me]
    for step in range(1, count):
        total = total + landed[step]
    out[me] = total
    loop(lambda step: spread(step).start())
    loop(lambda step: arrival(step).wait_recv())
    loop(lambda step: scatter(step).wait_send())
    loop(lambda step: spread(step).wait_send())


def panel_kernel(
    count, cores, part_ref, library_ref, scale_ref, vectors_ref, mixed_ref,
    part, landed, gathered, part_two, landed_two, gathered_two, halves,
    weights, work, inner, taus, row_sems, row_sems_two, core_sems, half_sems,
):
    me, core = lax.axis_index("rows"), lax.axis_index("grid")
    width, block = part_ref.shape
    per = width // count
    barrier = pltpu.get_barrier_semaphore()

    def greet(step, carry):
        pl.semaphore_signal(
            barrier, inc=1, device_id=(lax.rem(me + step, count), core), device_id_type=pl.DeviceIdType.MESH
        )
        return carry

    lax.fori_loop(1, count, greet, 0)
    for step in range(1, cores):
        pl.semaphore_signal(
            barrier, inc=1, device_id=(me, lax.rem(core + step, cores)), device_id_type=pl.DeviceIdType.MESH
        )
    for place in range(count):
        part[place] = part_ref[place * per:(place + 1) * per, :]
    pl.semaphore_wait(barrier, count + cores - 2)

    sum_rows(count, part, landed, gathered.at[core], [row_sems.at[k] for k in range(4)])
    shares = []
    for step in range(1, cores):
        peer = lax.rem(core + step, cores)
        shares.append(
            remote(gathered.at[core], gathered.at[core], core_sems.at[0, step], core_sems.at[1, step], (me, peer))
        )
        shares[-1].start()
    for step in range(1, cores):
        peer = lax.rem(core + cores - step, cores)
        remote(
            gathered.at[peer], gathered.at[peer], core_sems.at[0, step], core_sems.at[1, step], (me, peer)
        ).wait_recv()
    for share in shares:
        share.wait_send()
    for half in range(cores):
        for place in range(count):
            work[place * per:(place + 1) * per, half * block:(half + 1) * block] = gathered[half, place]

    reflect(vectors_ref, weights, work, inner, taus)

    step_cols = min(block, 512)
    halves[0] = jnp.zeros_like(halves[0])
    for start in range(0, block, step_cols):
        cols = slice(start, start + step_cols)
        own = weights[:, pl.ds(pl.multiple_of(core * block + start, 128), step_cols)] * scale_ref[:, cols]
        halves[0] += lax.dot_general(
            own, library_ref[:, cols].astype(jnp.float32), (((1,), (1,)), ((), ())),
            precision=HIGH, preferred_element_type=jnp.float32,
        )
    shares = []
    for step in range(1, cores):
        peer = lax.rem(core + step, cores)
        shares.append(
            remote(halves.at[0], halves.at[step], half_sems.at[0, step], half_sems.at[1, step], (me, peer))
        )
        shares[-1].start()
    for share in shares:
        share.wait()
    summed = halves[0]
    for step in range(1, cores):
        summed = summed + halves[step]
    for start in range(0, block, step_cols):
        cols = slice(start, start + step_cols)
        chunk = jnp.dot(
            summed, library_ref[:, cols].astype(jnp.float32), precision=HIGH, preferred_element_type=jnp.float32
        )
        for place in range(count):
            part_two[place, :, cols] = chunk[place * per:(place + 1) * per, :]
    sum_rows(count, part_two, landed_two, gathered_two, [row_sems_two.at[k] for k in range(4)])
    for place in range(count):
        mixed_ref[place * per:(place + 1) * per, :] = gathered_two[place] * scale_ref[...]


def panel_chain(part, library, scale, count, cores):
    width, block = part.shape
    rows_dev = library.shape[0]
    per = width // count
    size = block * cores
    real = jnp.float32
    slices = pltpu.VMEM((count, per, block), real)
    return pl.pallas_call(
        functools.partial(panel_kernel, count, cores),
        out_shape=(jax.ShapeDtypeStruct((width, size), real), jax.ShapeDtypeStruct((width, block), real)),
        in_specs=[pl.BlockSpec(memory_space=pltpu.VMEM)] * 3,
        out_specs=(pl.BlockSpec(memory_space=pltpu.VMEM),) * 2,
        scratch_shapes=[
            slices, slices, pltpu.VMEM((cores, count, per, block), real),
            slices, slices, slices, pltpu.VMEM((cores, width, rows_dev), real),
            pltpu.VMEM((width, size), real), pltpu.VMEM((width, size), real),
            pltpu.VMEM((width, width), real), pltpu.VMEM((width, 128), real),
            pltpu.SemaphoreType.DMA((4, count)), pltpu.SemaphoreType.DMA((4, count)),
            pltpu.SemaphoreType.DMA((2, cores)), pltpu.SemaphoreType.DMA((2, cores)),
        ],
        compiler_params=pltpu.CompilerParams(
            vmem_limit_bytes=32 << 20, collective_id=0, has_side_effects=True
        ),
        cost_estimate=pl.CostEstimate(flops=20_000_000_000, bytes_accessed=200_000_000, transcendentals=0),
    )(part, library, scale)


def per_device(library, col_scale):
    rows_dev, col_block = library.shape
    count_rows = lax.axis_size("rows")
    count_grid = lax.axis_size("grid")
    columns = col_block * count_grid
    row_block = columns // count_rows
    total = rows_dev * count_rows
    near = 1
    while near * near < count_rows:
        near *= 2
    far = count_rows // near
    grid_place = lax.axis_index("grid")
    rows_place = lax.axis_index("rows")
    near_groups = [[f * near + n for n in range(near)] for f in range(far)]
    far_groups = [[f * near + n for f in range(far)] for n in range(near)]
    own_scale = lax.dynamic_slice_in_dim(col_scale, grid_place * col_block, col_block)

    head = lax.all_gather(library[:, :PANEL], "grid", axis=0)[0]
    panel_part = lax.dot_general(
        head, library, (((0,), (0,)), ((), ())), preferred_element_type=jnp.float32
    )
    panel_part = panel_part * (col_scale[:PANEL, None] * own_scale[None, :] / total)
    vectors, mixed = panel_chain(panel_part, library, own_scale[None, :], count_rows, count_grid)
    mixed = mixed / total

    whole = lax.all_gather(library, "rows", axis=0, tiled=True, axis_index_groups=near_groups)
    place = rows_place % near
    blocks = whole.reshape(near * rows_dev, far // count_grid, near, row_block)
    left = lax.dynamic_index_in_dim(blocks, place, 2, keepdims=False)
    left = lax.all_gather(left, "grid", axis=1, tiled=True).reshape(near * rows_dev, far * row_block)
    product = lax.dot_general(
        left, whole, (((0,), (0,)), ((), ())), preferred_element_type=jnp.float32
    )
    gram = lax.psum_scatter(
        product, "rows", scatter_dimension=0, tiled=True, axis_index_groups=far_groups
    )
    row_scale = lax.dynamic_slice_in_dim(col_scale, rows_place * row_block, row_block)

    own_vectors = lax.dynamic_slice_in_dim(vectors, rows_place * row_block, row_block, 1).T
    gram = gram * (row_scale[:, None] * own_scale[None, :] / total)
    updated = gram - jnp.dot(own_vectors, mixed, precision=HIGH)
    return (updated, own_vectors)


def solution(mesh):
    return jax.shard_map(
        per_device,
        mesh=mesh,
        in_specs=(P("rows", "grid"), P()),
        out_specs=(P("rows", "grid"), P("rows", None)),
        check_vma=False,
    )
```

```python
import functools

import jax
import jax.numpy as jnp
from jax import lax
from jax.experimental import pallas as pl
from jax.experimental.pallas import tpu as pltpu
from jax.sharding import PartitionSpec as P

PANEL = 64
HIGH = lax.Precision.HIGHEST


def reflect(vectors_ref, weights_ref, work, inner, taus):
    width, size = work.shape
    lane = lax.broadcasted_iota(jnp.int32, (1, size), 1)
    for base in range(0, width, 8):

        def one_step(step, carry, base=base):
            place = base + step
            row = work[pl.ds(place, 1), :]
            row = jnp.where(lane >= place, row, 0.0)
            pivot = jnp.sum(jnp.where(lane == place, row, 0.0), axis=1, keepdims=True)
            length = jnp.sqrt(jnp.sum(row * row, axis=1, keepdims=True))
            signed = jnp.where(pivot >= 0.0, length, -length)
            vector = row + jnp.where(lane == place, signed, 0.0)
            tau = 1.0 / (length * (length + jnp.abs(pivot)))
            rest = work[base:, :]
            project = jnp.sum(rest * vector, axis=1, keepdims=True)
            work[base:, :] = rest - (tau * project) * vector
            vectors_ref[pl.ds(place, 1), :] = vector
            taus[pl.ds(place, 1), :] = jnp.broadcast_to(tau, (1, 128))
            return carry

        lax.fori_loop(0, 8, one_step, 0)
    vectors = vectors_ref[...]
    inner[...] = lax.dot_general(
        vectors, vectors, (((1,), (1,)), ((), ())), precision=HIGH, preferred_element_type=jnp.float32
    )
    across = lax.broadcasted_iota(jnp.int32, (width, width), 1)
    down = lax.broadcasted_iota(jnp.int32, (width, 1), 0)

    def factor_step(place, factor):
        tau = taus[pl.ds(place, 1), 0:1]
        coupling = jnp.where(across < place, inner[pl.ds(place, 1), :] * factor, 0.0)
        column = -tau * jnp.sum(coupling, axis=1, keepdims=True)
        column = column + jnp.where(down == place, tau, 0.0)
        return jnp.where(across == place, column, factor)

    factor = lax.fori_loop(0, width, factor_step, jnp.zeros((width, width), jnp.float32))
    weights_ref[...] = lax.dot_general(
        factor, vectors, (((0,), (0,)), ((), ())), precision=HIGH, preferred_element_type=jnp.float32
    )


def remote(source, target, send, recv, place):
    return pltpu.make_async_remote_copy(
        src_ref=source, dst_ref=target, send_sem=send, recv_sem=recv,
        device_id=place, device_id_type=pl.DeviceIdType.MESH,
    )


def sum_rows(count, part, landed, out, sems):
    me, core = lax.axis_index("rows"), lax.axis_index("grid")
    send, recv, send_back, recv_back = sems

    def scatter(step):
        peer = lax.rem(me + step, count)
        return remote(part.at[peer], landed.at[step], send.at[step], recv.at[step], (peer, core))

    def spread(step):
        peer = lax.rem(me + step, count)
        return remote(out.at[me], out.at[me], send_back.at[step], recv_back.at[step], (peer, core))

    def arrival(step):
        peer = lax.rem(me + count - step, count)
        return remote(out.at[peer], out.at[peer], send_back.at[step], recv_back.at[step], (peer, core))

    def loop(action):
        def body(step, carry):
            action(step)
            return carry
        lax.fori_loop(1, count, body, 0)

    loop(lambda step: scatter(step).start())
    loop(lambda step: scatter(step).wait_recv())
    total = part[me]
    for step in range(1, count):
        total = total + landed[step]
    out[me] = total
    loop(lambda step: spread(step).start())
    loop(lambda step: arrival(step).wait_recv())
    loop(lambda step: scatter(step).wait_send())
    loop(lambda step: spread(step).wait_send())


def panel_kernel(
    count, cores, near, aligned, part_ref, library_ref, scale_ref, vectors_ref, mixed_ref, whole_ref, left_ref,
    part, landed, gathered, part_two, landed_two, gathered_two, halves,
    weights, work, inner, taus, row_sems, row_sems_two, core_sems, half_sems,
    near_sems, own_sem, side_sems, left_sems,
):
    me, core = lax.axis_index("rows"), lax.axis_index("grid")
    width, block = part_ref.shape
    per = width // count
    barrier = pltpu.get_barrier_semaphore()

    def greet(step, carry):
        pl.semaphore_signal(
            barrier, inc=1, device_id=(lax.rem(me + step, count), core), device_id_type=pl.DeviceIdType.MESH
        )
        return carry

    lax.fori_loop(1, count, greet, 0)
    for step in range(1, cores):
        pl.semaphore_signal(
            barrier, inc=1, device_id=(me, lax.rem(core + step, cores)), device_id_type=pl.DeviceIdType.MESH
        )
    for place in range(count):
        part[place] = part_ref[place * per:(place + 1) * per, :]
    pl.semaphore_wait(barrier, count + cores - 2)

    place_near = lax.rem(me, near)
    first = me - place_near

    def to_peer(step):
        peer = lax.rem(place_near + step, near)
        return remote(
            library_ref, whole_ref.at[place_near], near_sems.at[0, step], near_sems.at[1, step], (first + peer, core)
        )

    def from_peer(step):
        peer = lax.rem(place_near + near - step, near)
        return remote(
            library_ref, whole_ref.at[peer], near_sems.at[0, step], near_sems.at[1, step], (first + peer, core)
        )

    keep = pltpu.make_async_copy(library_ref, whole_ref.at[place_near], own_sem)
    keep.start()
    for step in range(1, near):
        to_peer(step).start()

    sum_rows(count, part, landed, gathered.at[core], [row_sems.at[k] for k in range(4)])
    shares = []
    for step in range(1, cores):
        peer = lax.rem(core + step, cores)
        shares.append(
            remote(gathered.at[core], gathered.at[core], core_sems.at[0, step], core_sems.at[1, step], (me, peer))
        )
        shares[-1].start()
    for step in range(1, cores):
        peer = lax.rem(core + cores - step, cores)
        remote(
            gathered.at[peer], gathered.at[peer], core_sems.at[0, step], core_sems.at[1, step], (me, peer)
        ).wait_recv()
    for share in shares:
        share.wait_send()
    for half in range(cores):
        for place in range(count):
            work[place * per:(place + 1) * per, half * block:(half + 1) * block] = gathered[half, place]

    reflect(vectors_ref, weights, work, inner, taus)

    keep.wait()
    for step in range(1, near):
        from_peer(step).wait_recv()
        to_peer(step).wait_send()
    moves = []
    if aligned:
        far = count // near
        row_block = block * cores // count
        for piece in range(far // cores):
            offset = pl.multiple_of((piece * near + place_near) * row_block, 128)
            source = whole_ref.at[:, :, pl.ds(offset, row_block)]
            target = left_ref.at[core, piece]
            moves.append(pltpu.make_async_copy(source, target, left_sems.at[piece]))
            moves[-1].start()
            for step in range(1, cores):
                peer = lax.rem(core + step, cores)
                moves.append(
                    remote(source, target, side_sems.at[0, step, piece], side_sems.at[1, step, piece], (me, peer))
                )
                moves[-1].start()

    step_cols = min(block, 512)
    halves[0] = jnp.zeros_like(halves[0])
    for start in range(0, block, step_cols):
        cols = slice(start, start + step_cols)
        own = weights[:, pl.ds(pl.multiple_of(core * block + start, 128), step_cols)] * scale_ref[:, cols]
        halves[0] += lax.dot_general(
            own, library_ref[:, cols].astype(jnp.float32), (((1,), (1,)), ((), ())),
            precision=HIGH, preferred_element_type=jnp.float32,
        )
    shares = []
    for step in range(1, cores):
        peer = lax.rem(core + step, cores)
        shares.append(
            remote(halves.at[0], halves.at[step], half_sems.at[0, step], half_sems.at[1, step], (me, peer))
        )
        shares[-1].start()
    for share in shares:
        share.wait()
    summed = halves[0]
    for step in range(1, cores):
        summed = summed + halves[step]
    for start in range(0, block, step_cols):
        cols = slice(start, start + step_cols)
        chunk = jnp.dot(
            summed, library_ref[:, cols].astype(jnp.float32), precision=HIGH, preferred_element_type=jnp.float32
        )
        for place in range(count):
            part_two[place, :, cols] = chunk[place * per:(place + 1) * per, :]
    sum_rows(count, part_two, landed_two, gathered_two, [row_sems_two.at[k] for k in range(4)])
    for place in range(count):
        mixed_ref[place * per:(place + 1) * per, :] = gathered_two[place] * scale_ref[...]
    for move in moves:
        move.wait()


def panel_chain(part, library, scale, count, cores, near):
    width, block = part.shape
    rows_dev = library.shape[0]
    per = width // count
    size = block * cores
    real = jnp.float32
    slices = pltpu.VMEM((count, per, block), real)
    row_block = size // count
    aligned = row_block % 128 == 0
    pieces = count // near // cores
    return pl.pallas_call(
        functools.partial(panel_kernel, count, cores, near, aligned),
        out_shape=(
            jax.ShapeDtypeStruct((width, size), real),
            jax.ShapeDtypeStruct((width, block), real),
            jax.ShapeDtypeStruct((near, rows_dev, block), jnp.bfloat16),
            jax.ShapeDtypeStruct((cores, pieces, near, rows_dev, row_block), jnp.bfloat16),
        ),
        in_specs=[pl.BlockSpec(memory_space=pltpu.VMEM)] * 3,
        out_specs=(pl.BlockSpec(memory_space=pltpu.VMEM),) * 2 + (pl.BlockSpec(memory_space=pltpu.HBM),) * 2,
        scratch_shapes=[
            slices, slices, pltpu.VMEM((cores, count, per, block), real),
            slices, slices, slices, pltpu.VMEM((cores, width, rows_dev), real),
            pltpu.VMEM((width, size), real), pltpu.VMEM((width, size), real),
            pltpu.VMEM((width, width), real), pltpu.VMEM((width, 128), real),
            pltpu.SemaphoreType.DMA((4, count)), pltpu.SemaphoreType.DMA((4, count)),
            pltpu.SemaphoreType.DMA((2, cores)), pltpu.SemaphoreType.DMA((2, cores)),
            pltpu.SemaphoreType.DMA((2, near)), pltpu.SemaphoreType.DMA(()),
            pltpu.SemaphoreType.DMA((2, cores, pieces)), pltpu.SemaphoreType.DMA((pieces,)),
        ],
        compiler_params=pltpu.CompilerParams(
            vmem_limit_bytes=32 << 20, collective_id=0, has_side_effects=True
        ),
        cost_estimate=pl.CostEstimate(flops=20_000_000_000, bytes_accessed=200_000_000, transcendentals=0),
    )(part, library, scale)


def per_device(library, col_scale):
    rows_dev, col_block = library.shape
    count_rows = lax.axis_size("rows")
    count_grid = lax.axis_size("grid")
    columns = col_block * count_grid
    row_block = columns // count_rows
    total = rows_dev * count_rows
    near = 1
    while near * near < count_rows:
        near *= 2
    far = count_rows // near
    grid_place = lax.axis_index("grid")
    rows_place = lax.axis_index("rows")
    far_groups = [[f * near + n for f in range(far)] for n in range(near)]
    own_scale = lax.dynamic_slice_in_dim(col_scale, grid_place * col_block, col_block)

    head = lax.all_gather(library[:, :PANEL], "grid", axis=0)[0]
    panel_part = lax.dot_general(
        head, library, (((0,), (0,)), ((), ())), preferred_element_type=jnp.float32
    )
    panel_part = panel_part * (col_scale[:PANEL, None] * own_scale[None, :] / total)
    vectors, mixed, whole, left = panel_chain(
        panel_part, library, own_scale[None, :], count_rows, count_grid, near
    )
    mixed = mixed / total

    samples = near * rows_dev
    whole = whole.reshape(samples, col_block)
    if row_block % 128:
        blocks = whole.reshape(samples, far // count_grid, near, row_block)
        left = lax.dynamic_index_in_dim(blocks, rows_place % near, 2, keepdims=False)
        left = lax.all_gather(left, "grid", axis=1, tiled=True)
    else:
        left = left.reshape(far, samples, row_block).transpose(1, 0, 2)
    product = lax.dot_general(
        left, whole, (((0,), (0,)), ((), ())), preferred_element_type=jnp.float32
    ).reshape(far * row_block, col_block)
    gram = lax.psum_scatter(
        product, "rows", scatter_dimension=0, tiled=True, axis_index_groups=far_groups
    )
    row_scale = lax.dynamic_slice_in_dim(col_scale, rows_place * row_block, row_block)

    own_vectors = lax.dynamic_slice_in_dim(vectors, rows_place * row_block, row_block, 1).T
    gram = gram * (row_scale[:, None] * own_scale[None, :] / total)
    updated = gram - jnp.dot(own_vectors, mixed, precision=HIGH)
    return (updated, own_vectors)


def solution(mesh):
    return jax.shard_map(
        per_device,
        mesh=mesh,
        in_specs=(P("rows", "grid"), P()),
        out_specs=(P("rows", "grid"), P("rows", None)),
        check_vma=False,
    )
```

```python
import functools

import jax
import jax.numpy as jnp
from jax import lax
from jax.experimental import pallas as pl
from jax.experimental.pallas import tpu as pltpu
from jax.sharding import PartitionSpec as P

PANEL = 64
HIGH = lax.Precision.HIGHEST


def reflect(vectors_ref, weights_ref, work, inner, taus):
    width, size = work.shape
    lane = lax.broadcasted_iota(jnp.int32, (1, size), 1)
    for base in range(0, width, 8):

        def one_step(step, carry, base=base):
            place = base + step
            row = work[pl.ds(place, 1), :]
            row = jnp.where(lane >= place, row, 0.0)
            pivot = jnp.sum(jnp.where(lane == place, row, 0.0), axis=1, keepdims=True)
            length = jnp.sqrt(jnp.sum(row * row, axis=1, keepdims=True))
            signed = jnp.where(pivot >= 0.0, length, -length)
            vector = row + jnp.where(lane == place, signed, 0.0)
            tau = 1.0 / (length * (length + jnp.abs(pivot)))
            rest = work[base:, :]
            project = jnp.sum(rest * vector, axis=1, keepdims=True)
            work[base:, :] = rest - (tau * project) * vector
            vectors_ref[pl.ds(place, 1), :] = vector
            taus[pl.ds(place, 1), :] = jnp.broadcast_to(tau, (1, 128))
            return carry

        lax.fori_loop(0, 8, one_step, 0)
    vectors = vectors_ref[...]
    inner[...] = lax.dot_general(
        vectors, vectors, (((1,), (1,)), ((), ())), precision=HIGH, preferred_element_type=jnp.float32
    )
    across = lax.broadcasted_iota(jnp.int32, (width, width), 1)
    down = lax.broadcasted_iota(jnp.int32, (width, 1), 0)

    def factor_step(place, factor):
        tau = taus[pl.ds(place, 1), 0:1]
        coupling = jnp.where(across < place, inner[pl.ds(place, 1), :] * factor, 0.0)
        column = -tau * jnp.sum(coupling, axis=1, keepdims=True)
        column = column + jnp.where(down == place, tau, 0.0)
        return jnp.where(across == place, column, factor)

    factor = lax.fori_loop(0, width, factor_step, jnp.zeros((width, width), jnp.float32))
    weights_ref[...] = lax.dot_general(
        factor, vectors, (((0,), (0,)), ((), ())), precision=HIGH, preferred_element_type=jnp.float32
    )


def remote(source, target, send, recv, place):
    return pltpu.make_async_remote_copy(
        src_ref=source, dst_ref=target, send_sem=send, recv_sem=recv,
        device_id=place, device_id_type=pl.DeviceIdType.MESH,
    )


def sum_rows(count, part, landed, out, sems):
    me, core = lax.axis_index("rows"), lax.axis_index("grid")
    send, recv, send_back, recv_back = sems

    def scatter(step):
        peer = lax.rem(me + step, count)
        return remote(part.at[peer], landed.at[step], send.at[step], recv.at[step], (peer, core))

    def spread(step):
        peer = lax.rem(me + step, count)
        return remote(out.at[me], out.at[me], send_back.at[step], recv_back.at[step], (peer, core))

    def arrival(step):
        peer = lax.rem(me + count - step, count)
        return remote(out.at[peer], out.at[peer], send_back.at[step], recv_back.at[step], (peer, core))

    def loop(action):
        def body(step, carry):
            action(step)
            return carry
        lax.fori_loop(1, count, body, 0)

    loop(lambda step: scatter(step).start())
    loop(lambda step: scatter(step).wait_recv())
    total = part[me]
    for step in range(1, count):
        total = total + landed[step]
    out[me] = total
    loop(lambda step: spread(step).start())
    loop(lambda step: arrival(step).wait_recv())
    loop(lambda step: scatter(step).wait_send())
    loop(lambda step: spread(step).wait_send())


def panel_kernel(
    count, cores, part_ref, library_ref, scale_ref, vectors_ref, mixed_ref,
    part, landed, gathered, part_two, landed_two, gathered_two, halves,
    weights, work, inner, taus, row_sems, row_sems_two, core_sems, half_sems,
):
    me, core = lax.axis_index("rows"), lax.axis_index("grid")
    width, block = part_ref.shape
    per = width // count
    barrier = pltpu.get_barrier_semaphore()

    def greet(step, carry):
        pl.semaphore_signal(
            barrier, inc=1, device_id=(lax.rem(me + step, count), core), device_id_type=pl.DeviceIdType.MESH
        )
        return carry

    lax.fori_loop(1, count, greet, 0)
    for step in range(1, cores):
        pl.semaphore_signal(
            barrier, inc=1, device_id=(me, lax.rem(core + step, cores)), device_id_type=pl.DeviceIdType.MESH
        )
    for place in range(count):
        part[place] = part_ref[place * per:(place + 1) * per, :]
    pl.semaphore_wait(barrier, count + cores - 2)

    sum_rows(count, part, landed, gathered.at[core], [row_sems.at[k] for k in range(4)])
    shares = []
    for step in range(1, cores):
        peer = lax.rem(core + step, cores)
        shares.append(
            remote(gathered.at[core], gathered.at[core], core_sems.at[0, step], core_sems.at[1, step], (me, peer))
        )
        shares[-1].start()
    for step in range(1, cores):
        peer = lax.rem(core + cores - step, cores)
        remote(
            gathered.at[peer], gathered.at[peer], core_sems.at[0, step], core_sems.at[1, step], (me, peer)
        ).wait_recv()
    for share in shares:
        share.wait_send()
    for half in range(cores):
        for place in range(count):
            work[place * per:(place + 1) * per, half * block:(half + 1) * block] = gathered[half, place]

    reflect(vectors_ref, weights, work, inner, taus)

    step_cols = min(block, 512)
    halves[0] = jnp.zeros_like(halves[0])
    for start in range(0, block, step_cols):
        cols = slice(start, start + step_cols)
        own = weights[:, pl.ds(pl.multiple_of(core * block + start, 128), step_cols)] * scale_ref[:, cols]
        halves[0] += lax.dot_general(
            own, library_ref[:, cols].astype(jnp.float32), (((1,), (1,)), ((), ())),
            precision=HIGH, preferred_element_type=jnp.float32,
        )
    shares = []
    for step in range(1, cores):
        peer = lax.rem(core + step, cores)
        shares.append(
            remote(halves.at[0], halves.at[step], half_sems.at[0, step], half_sems.at[1, step], (me, peer))
        )
        shares[-1].start()
    for share in shares:
        share.wait()
    summed = halves[0]
    for step in range(1, cores):
        summed = summed + halves[step]
    for start in range(0, block, step_cols):
        cols = slice(start, start + step_cols)
        chunk = jnp.dot(
            summed, library_ref[:, cols].astype(jnp.float32), precision=HIGH, preferred_element_type=jnp.float32
        )
        for place in range(count):
            part_two[place, :, cols] = chunk[place * per:(place + 1) * per, :]
    sum_rows(count, part_two, landed_two, gathered_two, [row_sems_two.at[k] for k in range(4)])
    for place in range(count):
        mixed_ref[place * per:(place + 1) * per, :] = gathered_two[place] * scale_ref[...]


def panel_chain(part, library, scale, count, cores):
    width, block = part.shape
    rows_dev = library.shape[0]
    per = width // count
    size = block * cores
    real = jnp.float32
    slices = pltpu.VMEM((count, per, block), real)
    return pl.pallas_call(
        functools.partial(panel_kernel, count, cores),
        out_shape=(jax.ShapeDtypeStruct((width, size), real), jax.ShapeDtypeStruct((width, block), real)),
        in_specs=[pl.BlockSpec(memory_space=pltpu.VMEM)] * 3,
        out_specs=(pl.BlockSpec(memory_space=pltpu.VMEM),) * 2,
        scratch_shapes=[
            slices, slices, pltpu.VMEM((cores, count, per, block), real),
            slices, slices, slices, pltpu.VMEM((cores, width, rows_dev), real),
            pltpu.VMEM((width, size), real), pltpu.VMEM((width, size), real),
            pltpu.VMEM((width, width), real), pltpu.VMEM((width, 128), real),
            pltpu.SemaphoreType.DMA((4, count)), pltpu.SemaphoreType.DMA((4, count)),
            pltpu.SemaphoreType.DMA((2, cores)), pltpu.SemaphoreType.DMA((2, cores)),
        ],
        compiler_params=pltpu.CompilerParams(
            vmem_limit_bytes=32 << 20, collective_id=0, has_side_effects=True
        ),
        cost_estimate=pl.CostEstimate(flops=20_000_000_000, bytes_accessed=200_000_000, transcendentals=0),
    )(part, library, scale)


def per_device(library, col_scale):
    rows_dev, col_block = library.shape
    count_rows = lax.axis_size("rows")
    count_grid = lax.axis_size("grid")
    columns = col_block * count_grid
    row_block = columns // count_rows
    total = rows_dev * count_rows
    near = 1
    while near * near < count_rows:
        near *= 2
    far = count_rows // near
    grid_place = lax.axis_index("grid")
    rows_place = lax.axis_index("rows")
    near_groups = [[f * near + n for n in range(near)] for f in range(far)]
    far_groups = [[f * near + n for f in range(far)] for n in range(near)]
    own_scale = lax.dynamic_slice_in_dim(col_scale, grid_place * col_block, col_block)

    head = lax.all_gather(library[:, :PANEL], "grid", axis=0)[0]
    panel_part = lax.dot_general(
        head, library, (((0,), (0,)), ((), ())), preferred_element_type=jnp.float32
    )
    panel_part = panel_part * (col_scale[:PANEL, None] * own_scale[None, :] / total)
    vectors, mixed = panel_chain(panel_part, library, own_scale[None, :], count_rows, count_grid)
    mixed = mixed / total

    whole = lax.all_gather(library, "rows", axis=0, tiled=True, axis_index_groups=near_groups)
    whole, vectors, mixed = lax.optimization_barrier((whole, vectors, mixed))
    place = rows_place % near
    blocks = whole.reshape(near * rows_dev, far // count_grid, near, row_block)
    left = lax.dynamic_index_in_dim(blocks, place, 2, keepdims=False)
    left = lax.all_gather(left, "grid", axis=1, tiled=True).reshape(near * rows_dev, far * row_block)
    product = lax.dot_general(
        left, whole, (((0,), (0,)), ((), ())), preferred_element_type=jnp.float32
    )
    gram = lax.psum_scatter(
        product, "rows", scatter_dimension=0, tiled=True, axis_index_groups=far_groups
    )
    row_scale = lax.dynamic_slice_in_dim(col_scale, rows_place * row_block, row_block)

    own_vectors = lax.dynamic_slice_in_dim(vectors, rows_place * row_block, row_block, 1).T
    gram = gram * (row_scale[:, None] * own_scale[None, :] / total)
    updated = gram - jnp.dot(own_vectors, mixed, precision=HIGH)
    return (updated, own_vectors)


def solution(mesh):
    return jax.shard_map(
        per_device,
        mesh=mesh,
        in_specs=(P("rows", "grid"), P()),
        out_specs=(P("rows", "grid"), P("rows", None)),
        check_vma=False,
    )
```

```python
import functools

import jax
import jax.numpy as jnp
from jax import lax
from jax.experimental import pallas as pl
from jax.experimental.pallas import tpu as pltpu
from jax.sharding import PartitionSpec as P

PANEL = 64
HIGH = lax.Precision.HIGHEST


def reflect(vectors_ref, weights_ref, work, inner, taus):
    width, size = work.shape
    lane = lax.broadcasted_iota(jnp.int32, (1, size), 1)
    for base in range(0, width, 8):

        def one_step(step, carry, base=base):
            place = base + step
            row = work[pl.ds(place, 1), :]
            row = jnp.where(lane >= place, row, 0.0)
            pivot = jnp.sum(jnp.where(lane == place, row, 0.0), axis=1, keepdims=True)
            length = jnp.sqrt(jnp.sum(row * row, axis=1, keepdims=True))
            signed = jnp.where(pivot >= 0.0, length, -length)
            vector = row + jnp.where(lane == place, signed, 0.0)
            tau = 1.0 / (length * (length + jnp.abs(pivot)))
            rest = work[base:, :]
            project = jnp.sum(rest * vector, axis=1, keepdims=True)
            work[base:, :] = rest - (tau * project) * vector
            vectors_ref[pl.ds(place, 1), :] = vector
            taus[pl.ds(place, 1), :] = jnp.broadcast_to(tau, (1, 128))
            return carry

        lax.fori_loop(0, 8, one_step, 0)
    vectors = vectors_ref[...]
    inner[...] = lax.dot_general(
        vectors, vectors, (((1,), (1,)), ((), ())), precision=HIGH, preferred_element_type=jnp.float32
    )
    across = lax.broadcasted_iota(jnp.int32, (width, width), 1)
    down = lax.broadcasted_iota(jnp.int32, (width, 1), 0)

    def factor_step(place, factor):
        tau = taus[pl.ds(place, 1), 0:1]
        coupling = jnp.where(across < place, inner[pl.ds(place, 1), :] * factor, 0.0)
        column = -tau * jnp.sum(coupling, axis=1, keepdims=True)
        column = column + jnp.where(down == place, tau, 0.0)
        return jnp.where(across == place, column, factor)

    factor = lax.fori_loop(0, width, factor_step, jnp.zeros((width, width), jnp.float32))
    weights_ref[...] = lax.dot_general(
        factor, vectors, (((0,), (0,)), ((), ())), precision=HIGH, preferred_element_type=jnp.float32
    )


def remote(source, target, send, recv, place):
    return pltpu.make_async_remote_copy(
        src_ref=source, dst_ref=target, send_sem=send, recv_sem=recv,
        device_id=place, device_id_type=pl.DeviceIdType.MESH,
    )


def sum_rows(count, part, landed, out, sems):
    me, core = lax.axis_index("rows"), lax.axis_index("grid")
    send, recv, send_back, recv_back = sems

    def scatter(step):
        peer = lax.rem(me + step, count)
        return remote(part.at[peer], landed.at[step], send.at[step], recv.at[step], (peer, core))

    def spread(step):
        peer = lax.rem(me + step, count)
        return remote(out.at[me], out.at[me], send_back.at[step], recv_back.at[step], (peer, core))

    def arrival(step):
        peer = lax.rem(me + count - step, count)
        return remote(out.at[peer], out.at[peer], send_back.at[step], recv_back.at[step], (peer, core))

    def loop(action):
        def body(step, carry):
            action(step)
            return carry
        lax.fori_loop(1, count, body, 0)

    loop(lambda step: scatter(step).start())
    loop(lambda step: scatter(step).wait_recv())
    total = part[me]
    for step in range(1, count):
        total = total + landed[step]
    out[me] = total
    loop(lambda step: spread(step).start())
    loop(lambda step: arrival(step).wait_recv())
    loop(lambda step: scatter(step).wait_send())
    loop(lambda step: spread(step).wait_send())


def panel_kernel(
    count, cores, part_ref, library_ref, scale_ref, vectors_ref, mixed_ref,
    part, landed, gathered, part_two, landed_two, gathered_two, halves,
    weights, work, inner, taus, row_sems, row_sems_two, core_sems, half_sems,
):
    me, core = lax.axis_index("rows"), lax.axis_index("grid")
    width, block = part_ref.shape
    per = width // count
    barrier = pltpu.get_barrier_semaphore()

    def greet(step, carry):
        pl.semaphore_signal(
            barrier, inc=1, device_id=(lax.rem(me + step, count), core), device_id_type=pl.DeviceIdType.MESH
        )
        return carry

    lax.fori_loop(1, count, greet, 0)
    for step in range(1, cores):
        pl.semaphore_signal(
            barrier, inc=1, device_id=(me, lax.rem(core + step, cores)), device_id_type=pl.DeviceIdType.MESH
        )
    for place in range(count):
        part[place] = part_ref[place * per:(place + 1) * per, :]
    pl.semaphore_wait(barrier, count + cores - 2)

    sum_rows(count, part, landed, gathered.at[core], [row_sems.at[k] for k in range(4)])
    shares = []
    for step in range(1, cores):
        peer = lax.rem(core + step, cores)
        shares.append(
            remote(gathered.at[core], gathered.at[core], core_sems.at[0, step], core_sems.at[1, step], (me, peer))
        )
        shares[-1].start()
    for step in range(1, cores):
        peer = lax.rem(core + cores - step, cores)
        remote(
            gathered.at[peer], gathered.at[peer], core_sems.at[0, step], core_sems.at[1, step], (me, peer)
        ).wait_recv()
    for share in shares:
        share.wait_send()
    for half in range(cores):
        for place in range(count):
            work[place * per:(place + 1) * per, half * block:(half + 1) * block] = gathered[half, place]

    reflect(vectors_ref, weights, work, inner, taus)

    step_cols = min(block, 512)
    halves[0] = jnp.zeros_like(halves[0])
    for start in range(0, block, step_cols):
        cols = slice(start, start + step_cols)
        own = weights[:, pl.ds(pl.multiple_of(core * block + start, 128), step_cols)] * scale_ref[:, cols]
        halves[0] += lax.dot_general(
            own, library_ref[:, cols].astype(jnp.float32), (((1,), (1,)), ((), ())),
            precision=HIGH, preferred_element_type=jnp.float32,
        )
    shares = []
    for step in range(1, cores):
        peer = lax.rem(core + step, cores)
        shares.append(
            remote(halves.at[0], halves.at[step], half_sems.at[0, step], half_sems.at[1, step], (me, peer))
        )
        shares[-1].start()
    for share in shares:
        share.wait()
    summed = halves[0]
    for step in range(1, cores):
        summed = summed + halves[step]
    for start in range(0, block, step_cols):
        cols = slice(start, start + step_cols)
        chunk = jnp.dot(
            summed, library_ref[:, cols].astype(jnp.float32), precision=HIGH, preferred_element_type=jnp.float32
        )
        for place in range(count):
            part_two[place, :, cols] = chunk[place * per:(place + 1) * per, :]
    sum_rows(count, part_two, landed_two, gathered_two, [row_sems_two.at[k] for k in range(4)])
    for place in range(count):
        mixed_ref[place * per:(place + 1) * per, :] = gathered_two[place] * scale_ref[...]


def panel_chain(part, library, scale, count, cores):
    width, block = part.shape
    rows_dev = library.shape[0]
    per = width // count
    size = block * cores
    real = jnp.float32
    slices = pltpu.VMEM((count, per, block), real)
    return pl.pallas_call(
        functools.partial(panel_kernel, count, cores),
        out_shape=(jax.ShapeDtypeStruct((width, size), real), jax.ShapeDtypeStruct((width, block), real)),
        in_specs=[pl.BlockSpec(memory_space=pltpu.VMEM)] * 3,
        out_specs=(pl.BlockSpec(memory_space=pltpu.VMEM),) * 2,
        scratch_shapes=[
            slices, slices, pltpu.VMEM((cores, count, per, block), real),
            slices, slices, slices, pltpu.VMEM((cores, width, rows_dev), real),
            pltpu.VMEM((width, size), real), pltpu.VMEM((width, size), real),
            pltpu.VMEM((width, width), real), pltpu.VMEM((width, 128), real),
            pltpu.SemaphoreType.DMA((4, count)), pltpu.SemaphoreType.DMA((4, count)),
            pltpu.SemaphoreType.DMA((2, cores)), pltpu.SemaphoreType.DMA((2, cores)),
        ],
        compiler_params=pltpu.CompilerParams(
            vmem_limit_bytes=32 << 20, collective_id=0, has_side_effects=True
        ),
        cost_estimate=pl.CostEstimate(flops=20_000_000_000, bytes_accessed=200_000_000, transcendentals=0),
    )(part, library, scale)


def per_device(library, col_scale):
    rows_dev, col_block = library.shape
    count_rows = lax.axis_size("rows")
    count_grid = lax.axis_size("grid")
    columns = col_block * count_grid
    row_block = columns // count_rows
    total = rows_dev * count_rows
    near = 1
    while near * near < count_rows:
        near *= 2
    far = count_rows // near
    grid_place = lax.axis_index("grid")
    rows_place = lax.axis_index("rows")
    near_groups = [[f * near + n for n in range(near)] for f in range(far)]
    far_groups = [[f * near + n for f in range(far)] for n in range(near)]
    own_scale = lax.dynamic_slice_in_dim(col_scale, grid_place * col_block, col_block)

    head = lax.all_gather(library[:, :PANEL], "grid", axis=0)[0]
    panel_part = lax.dot_general(
        head, library, (((0,), (0,)), ((), ())), preferred_element_type=jnp.float32
    )
    panel_part = panel_part * (col_scale[:PANEL, None] * own_scale[None, :] / total)
    vectors, mixed = panel_chain(panel_part, library, own_scale[None, :], count_rows, count_grid)
    mixed = mixed / total

    whole = lax.all_gather(library, "rows", axis=0, tiled=True, axis_index_groups=near_groups)
    whole, vectors, mixed = lax.optimization_barrier((whole, vectors, mixed))
    place = rows_place % near
    blocks = whole.T.reshape(far // count_grid, near, row_block, near * rows_dev)
    left = lax.dynamic_index_in_dim(blocks, place, 1, keepdims=False)
    left = left.reshape(far // count_grid * row_block, near * rows_dev)
    left = lax.all_gather(left, "grid", axis=0, tiled=True)
    product = lax.dot_general(
        left, whole, (((1,), (0,)), ((), ())), preferred_element_type=jnp.float32
    )
    gram = lax.psum_scatter(
        product, "rows", scatter_dimension=0, tiled=True, axis_index_groups=far_groups
    )
    row_scale = lax.dynamic_slice_in_dim(col_scale, rows_place * row_block, row_block)

    own_vectors = lax.dynamic_slice_in_dim(vectors, rows_place * row_block, row_block, 1).T
    gram = gram * (row_scale[:, None] * own_scale[None, :] / total)
    updated = gram - jnp.dot(own_vectors, mixed, precision=HIGH)
    return (updated, own_vectors)


def solution(mesh):
    return jax.shard_map(
        per_device,
        mesh=mesh,
        in_specs=(P("rows", "grid"), P()),
        out_specs=(P("rows", "grid"), P("rows", None)),
        check_vma=False,
    )
```
